32 devices in a mesh: groups: 2 (over x), expert: 16 (over z, y, core).
Axes of the slice: x: 2, y: 2, z: 4, core: 2. Of those that a mesh axis runs over, the one named last changes fastest.
Arguments:
- tokens: bfloat16 [4096, 2048], P(('groups', 'expert')), parts along dimension 0, may hold values from -6 to 6
- out_grad: bfloat16 [4096, 2048], P(('groups', 'expert')), parts along dimension 0, may hold values from -6 to 6
- gate_probs: float32 [4096, 8], P(('groups', 'expert')), parts along dimension 0, may hold values from 0.05 to 0.2
- routes: int32 [4096, 8], P(('groups', 'expert')), parts along dimension 0, may hold values from 0 to 15, all different within a row; in each aligned block of 128 rows (0 to 127, 128 to 255, ...) at most 80 rows name the same one
- w_gate: bfloat16 [16, 2048, 384], P('expert'), may hold values from -0.125 to 0.125
- w_up: bfloat16 [16, 2048, 384], P('expert'), may hold values from -0.125 to 0.125
- w_down: bfloat16 [16, 384, 2048], P('expert'), may hold values from -0.3125 to 0.3125
Outputs:
- tokens_grad: bfloat16 [4096, 2048], P(('groups', 'expert')), parts along dimension 0
- gate_wgrad: bfloat16 [32, 2048, 384], P(('groups', 'expert')), parts along dimension 0
- up_wgrad: bfloat16 [32, 2048, 384], P(('groups', 'expert')), parts along dimension 0
- down_wgrad: bfloat16 [32, 384, 2048], P(('groups', 'expert')), parts along dimension 0
The draws below stay inside these ranges and needn't reach their ends.
There are 2 independent parts, one for each index of `groups`. The reference program is written for one: setup_inputs(seed, part) draws one part's arguments, and reference() takes and returns one part's arrays. A program takes and returns all parts, laid end to end along the dimension named above; an argument that names none is the same for every part. Nothing has to cross between parts.
Inputs may be any that keep to these rules, and one draw needn't show every extreme that they name: A token's 8 experts differ. Among the 128 tokens of one block no expert is named by more than 80 routes, and in some block one expert is named by exactly 80.
All inputs are finite; a program needn't handle non-finite values.
Results may differ from the reference program's by a relative error of at most 0.0064.
Values may be sent and summed in bfloat16 or wider, within the bound.
No kernel may reach another device: no remote copies, remote signals or barrier semaphores. Data moves between devices by JAX's collectives and lax.ppermute only.
A program may use at most 128 MiB of HBM per device.

```python
import math
import jax
import jax.numpy as jnp
import numpy as np
from jax import lax

D = 2048
FF = 384
TOPK = 8
TOK_DEV = 128
EXPERTS = 16
TOKENS = 2048
CAP = 80
N_EXPERT = 16


def block_scale(own_key, extent, cuts, least, top_value):
    def one(dim, blocks):
        heights = jax.random.uniform(jax.random.fold_in(jax.random.fold_in(own_key, 6), dim), (blocks,), jnp.float32, least / len(cuts), top_value / len(cuts))
        return jnp.repeat(jnp.exp(heights), extent[dim] // blocks).reshape((-1,) + (1,) * (len(extent) - dim - 1))

    gain = one(*cuts[0])
    for cut in cuts[1:]:
        gain = gain * one(*cut)
    return gain


def routed_block(stream_key, own, number, rows, number_of, top, reach, lean):
    ranking = jax.random.permutation(stream_key, number_of)
    heavy_load, usual = load_shares(number_of, rows * top, reach, lean, True), load_shares(number_of, rows * top, reach, lean, False)
    places = jnp.arange(number_of)

    def named(tallies, rotation):
        used = int((tallies > 0).sum())
        fixed = max(1, used // 4)
        moved = fixed + (places - fixed + rotation * (used - fixed)) % max(1, number_of - fixed)
        return jnp.zeros((number_of,), jnp.int32).at[ranking[jnp.where(places < fixed, places, moved)]].set(jnp.asarray(tallies, jnp.int32))

    tallies = jnp.where(number % 4 == 0, named(heavy_load, number // 4), named(usual, number - number // 4 - 1))
    mixed = jax.random.permutation(jax.random.fold_in(own, 3), number_of)
    source_of, receiver = mixed[0:number_of // 2 * 2:2], mixed[1:number_of // 2 * 2:2]
    margin = jnp.minimum(tallies[source_of] - 1, reach - tallies[receiver]) // 2
    margin = jnp.where((source_of == ranking[0]) | (receiver == ranking[0]) | (tallies[receiver] == 0), 0, jnp.maximum(margin, 0))
    moved = jax.random.randint(jax.random.fold_in(own, 4), (number_of // 2,), 0, 1 << 20) % (margin + 1)
    tallies = tallies.at[source_of].add(-moved).at[receiver].add(moved)
    labels = jnp.searchsorted(jnp.cumsum(tallies), jnp.arange(rows * top), side="right").astype(jnp.int32)
    table = labels.reshape(top, rows).T
    table = table[jax.random.permutation(jax.random.fold_in(own, 1), rows)]
    rotation = jax.random.randint(jax.random.fold_in(own, 2), (rows, 1), 0, top)
    return jnp.take_along_axis(table, (jnp.arange(top)[None, :] + rotation) % top, axis=1)


def load_shares(number_of, total, reach, slope, full):
    weights = [(1 << 20) // math.isqrt(standing ** slope) + 1 for standing in range(1, number_of + 1)]
    largest = reach if full else min(reach, max(-(-total // number_of), total * weights[0] // sum(weights)))
    least = 1 if total - largest >= number_of - 1 else 0
    counts, surplus = [largest] + [least] * (number_of - 1), total - largest - least * (number_of - 1)
    while surplus > 0:
        candidates = [i for i in range(1, number_of) if counts[i] < largest] or [i for i in range(1, number_of) if counts[i] < reach]
        mass, left = sum([weights[i] for i in candidates]), surplus
        for i in candidates:
            addition = min(reach - counts[i], max(1, left * weights[i] // mass), surplus)
            counts[i] = counts[i] + addition
            surplus = surplus - addition
    return np.array(counts)


def centred(stream_key, extent, width, reach, cuts=(), kind=jnp.bfloat16):
    entries = jax.random.normal(stream_key, extent, jnp.float32) * width
    if len(cuts) > 0:
        entries = block_scale(stream_key, extent, cuts, -0.22, 0.18) * entries
    return jnp.clip(entries, min=-reach, max=reach).astype(kind)


def setup_inputs(seed: int = 0, part: int = 0) -> dict:
    arg_keys = jax.random.split(jax.random.key(seed), 8)
    part_splits = jax.random.split(jax.random.fold_in(arg_keys[7], part), 8)
    tokens = centred(part_splits[0], (TOKENS, D), 1.0, 6.0, ((0, 16),))
    out_grad = centred(part_splits[1], (TOKENS, D), 1.0, 6.0, ((0, 16),))
    gate_probs = jnp.clip(0.05 + 0.15 * jax.random.uniform(part_splits[2], (TOKENS, TOPK), jnp.float32) ** block_scale(part_splits[2], (TOKENS, TOPK), ((0, 16),), -0.2, 0.2), 0.05, 0.2)
    routes_keys = jax.random.split(jax.random.fold_in(part_splits[3], 1), TOKENS // TOK_DEV)
    routes_turns = jax.random.permutation(jax.random.fold_in(part_splits[3], 3), TOKENS // TOK_DEV)
    routes = jax.vmap(lambda own, number: routed_block(jax.random.fold_in(part_splits[3], 2), own, number, TOK_DEV, EXPERTS, TOPK, CAP, 2))(routes_keys, routes_turns).reshape((TOKENS, TOPK))
    w_gate = centred(arg_keys[4], (EXPERTS, D, FF), D ** -0.5, 0.125, ((0, 16),))
    w_up = centred(arg_keys[5], (EXPERTS, D, FF), D ** -0.5, 0.125, ((0, 16),))
    w_down = centred(arg_keys[6], (EXPERTS, FF, D), FF ** -0.5, 0.3125, ((0, 16),))
    return dict(tokens=tokens, out_grad=out_grad, gate_probs=gate_probs, routes=routes, w_gate=w_gate, w_up=w_up, w_down=w_down)


def expert_rows(inputs, grads_in, weight_gate, weight_up, weight_down):
    gate_pre = jnp.dot(inputs, weight_gate, preferred_element_type=jnp.float32)
    up_pre = jnp.dot(inputs, weight_up, preferred_element_type=jnp.float32)
    sigmoid_gate = jax.nn.sigmoid(gate_pre)
    activated = gate_pre * sigmoid_gate
    hidden = (activated * up_pre).astype(jnp.bfloat16)
    hidden_grad = jnp.dot(grads_in, weight_down.T, preferred_element_type=jnp.float32)
    up_grad = (hidden_grad * activated).astype(jnp.bfloat16)
    gate_grad = (hidden_grad * up_pre * sigmoid_gate * (1.0 + gate_pre * (1.0 - sigmoid_gate))).astype(jnp.bfloat16)
    row_grad = (jnp.dot(gate_grad, weight_gate.T, preferred_element_type=jnp.float32)
                + jnp.dot(up_grad, weight_up.T, preferred_element_type=jnp.float32)).astype(jnp.bfloat16)
    return hidden, gate_grad, up_grad, row_grad


def slot_numbers(expert_ids, experts):
    onehot = (expert_ids[:, None] == jnp.arange(experts, dtype=jnp.int32)[None, :]).astype(jnp.int32)
    running = jnp.cumsum(onehot, axis=0, dtype=jnp.int32)
    return (jnp.sum(running * onehot, axis=1, dtype=jnp.int32) - 1).astype(jnp.int32)


def reference(tokens, out_grad, gate_probs, routes, w_gate, w_up, w_down):
    experts = EXPERTS
    sources = N_EXPERT
    per_source = TOK_DEV * TOPK
    expert_ids = routes.reshape(sources, per_source).astype(jnp.int32)
    slots = jax.vmap(lambda ids: slot_numbers(ids, experts))(expert_ids)
    source_ids = (jnp.arange(sources * per_source, dtype=jnp.int32) // per_source).reshape(sources, per_source)
    places = ((source_ids * experts + expert_ids) * CAP + slots).reshape(-1).astype(jnp.int32)
    route_inputs = jnp.repeat(tokens, TOPK, axis=0)
    route_grads = (gate_probs[:, :, None] * out_grad[:, None, :].astype(jnp.float32)).astype(jnp.bfloat16).reshape(-1, D)
    buffer_in = jnp.zeros((sources * experts * CAP, D), jnp.bfloat16).at[places].set(route_inputs)
    buffer_grad = jnp.zeros((sources * experts * CAP, D), jnp.bfloat16).at[places].set(route_grads)
    buffer_in = buffer_in.reshape(sources, experts, CAP, D).transpose(1, 0, 2, 3).reshape(experts, sources * CAP, D)
    buffer_grad = buffer_grad.reshape(sources, experts, CAP, D).transpose(1, 0, 2, 3).reshape(experts, sources * CAP, D)

    def per_expert(items):
        inputs, grads_in, weight_gate, weight_up, weight_down = items
        hidden, gate_grad, up_grad, row_grad = expert_rows(inputs, grads_in, weight_gate, weight_up, weight_down)
        gate_w = jnp.dot(inputs.T, gate_grad, preferred_element_type=jnp.float32).astype(jnp.bfloat16)
        up_w = jnp.dot(inputs.T, up_grad, preferred_element_type=jnp.float32).astype(jnp.bfloat16)
        down_w = jnp.dot(hidden.T, grads_in, preferred_element_type=jnp.float32).astype(jnp.bfloat16)
        return row_grad, gate_w, up_w, down_w

    row_grads, gate_wgrad, up_wgrad, down_wgrad = lax.map(per_expert, (buffer_in, buffer_grad, w_gate, w_up, w_down))
    returned = row_grads.reshape(experts, sources, CAP, D).transpose(1, 0, 2, 3).reshape(-1, D)
    gathered = returned[places].reshape(TOKENS, TOPK, D)
    tokens_grad = jnp.sum(gathered, axis=1, dtype=jnp.float32).astype(jnp.bfloat16)
    return tokens_grad, gate_wgrad, up_wgrad, down_wgrad
```

```python
import functools

import jax
import jax.numpy as jnp
from jax import lax
from jax.experimental import pallas as pl
from jax.experimental.pallas import tpu as pltpu
from jax.sharding import PartitionSpec as P

F32 = jnp.float32
BF16 = jnp.bfloat16
NN = (((1,), (0,)), ((), ()))
NT = (((1,), (1,)), ((), ()))
TN = (((0,), (0,)), ((), ()))
GROUP = 4
PARTS = 3
BLOCK_VMEM = 16 << 20
WGRAD_VMEM = 24 << 20


def mm(a, b, dims):
    return lax.dot_general(a, b, dims, preferred_element_type=F32)


def near(v):
    return pltpu.with_memory_space_constraint(v, pltpu.VMEM)


def encode(probs):
    parts = []
    rest = probs
    for _ in range(PARTS):
        top = lax.reduce_precision(rest, 8, 7)
        parts.append(top.astype(BF16))
        rest = rest - top
    coded = jnp.concatenate(parts, axis=1)
    return jnp.pad(coded, ((0, 0), (0, -coded.shape[1] % 128)))


def block_pair(me, devices, xa, xb, oa, ob, wgu, wd):
    rows, width = oa.shape
    ff = wd.shape[0]

    def body(me, xa, xb, oa, ob, wgu, wd, row_a, row_b, grads, hidden):
        x = jnp.concatenate([xa[:, :width], xb[:, :width]], axis=0)
        o = jnp.concatenate([oa[...], ob[...]], axis=0)
        coded = jnp.concatenate([xa[:, width:], xb[:, width:]], axis=0).astype(F32)
        lane = lax.broadcasted_iota(jnp.int32, coded.shape, 1)
        mine = (lane % devices == me[0]) & (lane < PARTS * devices)
        p = jnp.sum(jnp.where(mine, coded, 0.0), axis=1, keepdims=True)
        pre = mm(x, wgu[...], NN)
        gate, up = pre[:, :ff], pre[:, ff:]
        hid = p * mm(o, wd[...], NT)
        sig = jax.nn.sigmoid(gate)
        act = gate * sig
        hidden[...] = (p * (act * up)).astype(BF16)
        grads[:, :ff] = (hid * up * sig * (1.0 + gate * (1.0 - sig))).astype(BF16)
        grads[:, ff:] = (hid * act).astype(BF16)
        back = mm(grads[...], wgu[...], NT).astype(BF16)
        row_a[...] = back[:rows]
        row_b[...] = back[rows:]

    return pl.pallas_call(
        body,
        in_specs=[pl.BlockSpec(memory_space=pltpu.SMEM)]
        + [pl.BlockSpec(memory_space=pltpu.VMEM)] * 6,
        out_shape=[
            jax.ShapeDtypeStruct((rows, width), BF16),
            jax.ShapeDtypeStruct((rows, width), BF16),
            jax.ShapeDtypeStruct((2 * rows, 2 * ff), BF16),
            jax.ShapeDtypeStruct((2 * rows, ff), BF16),
        ],
        compiler_params=pltpu.CompilerParams(vmem_limit_bytes=BLOCK_VMEM),
        cost_estimate=pl.CostEstimate(
            flops=2 * (2 * rows) * width * ff * 5,
            bytes_accessed=2 * (6 * rows * width + 3 * width * ff),
            transcendentals=2 * rows * ff,
        ),
        name="block_pair",
    )(me, near(xa), near(xb), near(oa), near(ob), near(wgu), near(wd))


def wgrad_group(xs, os, grads, hiddens, acc, last, resident):
    count, pairs = len(xs), len(grads)
    rows, width = os[0].shape
    ff = hiddens[0].shape[1]
    chunk = 512 if resident else 256
    has = acc is not None

    def body(*refs):
        start = pl.multiple_of(pl.program_id(0) * chunk, chunk)
        columns = pl.ds(start, chunk) if resident else slice(None)
        x = jnp.concatenate([r[:, columns] for r in refs[:count]], axis=0)
        o = jnp.concatenate([r[:, columns] for r in refs[count : 2 * count]], axis=0)
        rest = refs[2 * count :]
        g = jnp.concatenate([r[...] for r in rest[:pairs]], axis=0)
        h = jnp.concatenate([r[...] for r in rest[pairs : 2 * pairs]], axis=0)
        rest = rest[2 * pairs :]
        gu = mm(x, g, TN)
        dn = mm(h, o, TN)
        parts = [gu[:, :ff], gu[:, ff:], dn]
        if has:
            parts = [a[...] + b for a, b in zip(rest[:3], parts)]
            rest = rest[3:]
        for r, v in zip(rest, parts):
            r[...] = v.astype(r.dtype)

    tall = pl.BlockSpec((chunk, ff), lambda j: (j, 0))
    wide = pl.BlockSpec((ff, chunk), lambda j: (0, j))
    kind = BF16 if last else F32
    acc_specs = [tall, tall, wide]
    if resident:
        inputs = [near(v) for v in (*xs, *os, *grads, *hiddens)]
        specs = [pl.BlockSpec(memory_space=pltpu.VMEM)] * len(inputs)
    else:
        inputs = [*xs, *os, *grads, *hiddens]
        specs = [pl.BlockSpec((rows, chunk), lambda j: (0, j))] * (2 * count)
        specs += [pl.BlockSpec(v.shape, lambda j: (0, 0)) for v in (*grads, *hiddens)]
    alias = {len(inputs) + i: i for i in range(3)} if has and not last else {}
    return pl.pallas_call(
        body,
        grid=(width // chunk,),
        in_specs=specs + (acc_specs if has else []),
        out_specs=acc_specs,
        out_shape=[
            jax.ShapeDtypeStruct((width, ff), kind),
            jax.ShapeDtypeStruct((width, ff), kind),
            jax.ShapeDtypeStruct((ff, width), kind),
        ],
        input_output_aliases=alias,
        compiler_params=pltpu.CompilerParams(vmem_limit_bytes=WGRAD_VMEM),
        cost_estimate=pl.CostEstimate(
            flops=2 * count * rows * width * ff * 3,
            bytes_accessed=2 * 2 * count * rows * width + 4 * 3 * width * ff,
            transcendentals=0,
        ),
        name="wgrad_group",
    )(*inputs, *(acc if has else ()))


def chip_ring(chips, ladder):
    if ladder:
        return list(range(0, chips, 2)) + list(range(chips - 1, 0, -2))
    return list(range(chips))


def local(ladder, tokens, out_grad, gate_probs, routes, w_gate, w_up, w_down):
    devices = lax.axis_size("expert")
    chips = devices // 2
    resident = chips <= 8
    ring = chip_ring(chips, ladder)
    hop = [(2 * ring[i], 2 * ring[(i + 1) % chips]) for i in range(chips)]
    hop += [(2 * ring[(i + 1) % chips] + 1, 2 * ring[i] + 1) for i in range(chips)]
    swap = [(i, i ^ 1) for i in range(devices)]

    def forward(v):
        return lax.ppermute(v, "expert", hop)

    def other(v):
        return lax.ppermute(v, "expert", swap)

    me = lax.axis_index("expert").reshape(1)
    expert_ids = jnp.arange(devices, dtype=jnp.int32)
    named = routes[:, :, None] == expert_ids[None, None, :]
    probs = jnp.sum(jnp.where(named, gate_probs[:, :, None], 0.0), axis=1)
    x = jnp.concatenate([tokens, encode(probs)], axis=1)
    o = out_grad
    wgu = jnp.concatenate([w_gate[0], w_up[0]], axis=1)
    wd = w_down[0]

    acc, total, own = None, None, None
    held = []
    for s in range(chips):
        if s:
            x, o = forward(x), forward(o)
        xo, oo = other(x), other(o)
        row_a, row_b, grads, hidden = block_pair(me, devices, x, xo, o, oo, wgu, wd)
        partial = row_a.astype(F32) + other(row_b).astype(F32)
        if s == 0:
            own = partial
        else:
            if total is not None:
                partial = forward(total).astype(F32) + partial
            total = partial.astype(BF16)
        held.append((x, xo, o, oo, grads, hidden))
        if len(held) == GROUP or s == chips - 1:
            acc = wgrad_group(
                [v for h in held for v in h[:2]],
                [v for h in held for v in h[2:4]],
                [h[4] for h in held],
                [h[5] for h in held],
                acc,
                s == chips - 1,
                resident,
            )
            held = []
            if not resident:
                x, o, acc = lax.optimization_barrier((x, o, acc))
    total = forward(total).astype(F32) + own if chips > 1 else own
    gate_wgrad, up_wgrad, down_wgrad = acc
    return (
        total.astype(BF16),
        gate_wgrad[None],
        up_wgrad[None],
        down_wgrad[None],
    )


def solution(mesh):
    ladder = mesh.shape["groups"] == 2
    rows = P(("groups", "expert"), None)
    weights = P("expert", None, None)
    wgrads = P(("groups", "expert"), None, None)
    return jax.shard_map(
        functools.partial(local, ladder),
        mesh=mesh,
        in_specs=(rows, rows, rows, rows, weights, weights, weights),
        out_specs=(rows, wgrads, wgrads, wgrads),
        check_vma=False,
    )
```

```python
import functools

import jax
import jax.numpy as jnp
from jax import lax
from jax.experimental import pallas as pl
from jax.experimental.pallas import tpu as pltpu
from jax.sharding import PartitionSpec as P

F32 = jnp.float32
BF16 = jnp.bfloat16
NN = (((1,), (0,)), ((), ()))
NT = (((1,), (1,)), ((), ()))
TN = (((0,), (0,)), ((), ()))
GROUP = 4
PARTS = 3
BLOCK_VMEM = 16 << 20
WGRAD_VMEM = 24 << 20


def mm(a, b, dims):
    return lax.dot_general(a, b, dims, preferred_element_type=F32)


def near(v):
    return pltpu.with_memory_space_constraint(v, pltpu.VMEM)


def encode(probs):
    parts = []
    rest = probs
    for _ in range(PARTS):
        top = lax.reduce_precision(rest, 8, 7)
        parts.append(top.astype(BF16))
        rest = rest - top
    coded = jnp.concatenate(parts, axis=1)
    return jnp.pad(coded, ((0, 0), (0, -coded.shape[1] % 128)))


def block_pair(me, devices, xa, xb, oa, ob, wgu, wd):
    rows, width = oa.shape
    ff = wd.shape[0]

    def body(me, xa, xb, oa, ob, wgu, wd, row_a, row_b, grads, hidden):
        x = jnp.concatenate([xa[:, :width], xb[:, :width]], axis=0)
        o = jnp.concatenate([oa[...], ob[...]], axis=0)
        coded = jnp.concatenate([xa[:, width:], xb[:, width:]], axis=0).astype(F32)
        lane = lax.broadcasted_iota(jnp.int32, coded.shape, 1)
        mine = (lane % devices == me[0]) & (lane < PARTS * devices)
        p = jnp.sum(jnp.where(mine, coded, 0.0), axis=1, keepdims=True)
        pre = mm(x, wgu[...], NN)
        gate, up = pre[:, :ff], pre[:, ff:]
        hid = mm((p * o.astype(F32)).astype(BF16), wd[...], NT)
        sig = jax.nn.sigmoid(gate)
        act = gate * sig
        hidden[...] = (p * (act * up)).astype(BF16)
        grads[:, :ff] = (hid * up * sig * (1.0 + gate * (1.0 - sig))).astype(BF16)
        grads[:, ff:] = (hid * act).astype(BF16)
        back = mm(grads[...], wgu[...], NT).astype(BF16)
        row_a[...] = back[:rows]
        row_b[...] = back[rows:]

    return pl.pallas_call(
        body,
        in_specs=[pl.BlockSpec(memory_space=pltpu.SMEM)]
        + [pl.BlockSpec(memory_space=pltpu.VMEM)] * 6,
        out_shape=[
            jax.ShapeDtypeStruct((rows, width), BF16),
            jax.ShapeDtypeStruct((rows, width), BF16),
            jax.ShapeDtypeStruct((2 * rows, 2 * ff), BF16),
            jax.ShapeDtypeStruct((2 * rows, ff), BF16),
        ],
        compiler_params=pltpu.CompilerParams(vmem_limit_bytes=BLOCK_VMEM),
        cost_estimate=pl.CostEstimate(
            flops=2 * (2 * rows) * width * ff * 20,
            bytes_accessed=2 * (6 * rows * width + 3 * width * ff),
            transcendentals=2 * rows * ff,
        ),
        name="block_pair",
    )(me, near(xa), near(xb), near(oa), near(ob), near(wgu), near(wd))


def wgrad_group(xs, os, grads, hiddens, acc, last, resident):
    count, pairs = len(xs), len(grads)
    rows, width = os[0].shape
    ff = hiddens[0].shape[1]
    chunk = 512 if resident else 256
    has = acc is not None

    def body(*refs):
        start = pl.multiple_of(pl.program_id(0) * chunk, chunk)
        columns = pl.ds(start, chunk) if resident else slice(None)
        x = jnp.concatenate([r[:, columns] for r in refs[:count]], axis=0)
        o = jnp.concatenate([r[:, columns] for r in refs[count : 2 * count]], axis=0)
        rest = refs[2 * count :]
        g = jnp.concatenate([r[...] for r in rest[:pairs]], axis=0)
        h = jnp.concatenate([r[...] for r in rest[pairs : 2 * pairs]], axis=0)
        rest = rest[2 * pairs :]
        gu = mm(x, g, TN)
        dn = mm(h, o, TN)
        parts = [gu[:, :ff], gu[:, ff:], dn]
        if has:
            parts = [a[...] + b for a, b in zip(rest[:3], parts)]
            rest = rest[3:]
        for r, v in zip(rest, parts):
            r[...] = v.astype(r.dtype)

    tall = pl.BlockSpec((chunk, ff), lambda j: (j, 0))
    wide = pl.BlockSpec((ff, chunk), lambda j: (0, j))
    kind = BF16 if last else F32
    acc_specs = [tall, tall, wide]
    if resident:
        inputs = [near(v) for v in (*xs, *os, *grads, *hiddens)]
        specs = [pl.BlockSpec(memory_space=pltpu.VMEM)] * len(inputs)
    else:
        inputs = [*xs, *os, *grads, *hiddens]
        specs = [pl.BlockSpec((rows, chunk), lambda j: (0, j))] * (2 * count)
        specs += [pl.BlockSpec(v.shape, lambda j: (0, 0)) for v in (*grads, *hiddens)]
    alias = {len(inputs) + i: i for i in range(3)} if has and not last else {}
    return pl.pallas_call(
        body,
        grid=(width // chunk,),
        in_specs=specs + (acc_specs if has else []),
        out_specs=acc_specs,
        out_shape=[
            jax.ShapeDtypeStruct((width, ff), kind),
            jax.ShapeDtypeStruct((width, ff), kind),
            jax.ShapeDtypeStruct((ff, width), kind),
        ],
        input_output_aliases=alias,
        compiler_params=pltpu.CompilerParams(vmem_limit_bytes=WGRAD_VMEM),
        cost_estimate=pl.CostEstimate(
            flops=2 * count * rows * width * ff * 3,
            bytes_accessed=2 * 2 * count * rows * width + 4 * 3 * width * ff,
            transcendentals=0,
        ),
        name="wgrad_group",
    )(*inputs, *(acc if has else ()))


def chip_ring(chips, ladder):
    if ladder:
        return list(range(0, chips, 2)) + list(range(chips - 1, 0, -2))
    return list(range(chips))


def local(ladder, tokens, out_grad, gate_probs, routes, w_gate, w_up, w_down):
    devices = lax.axis_size("expert")
    chips = devices // 2
    resident = chips <= 8
    ring = chip_ring(chips, ladder)
    hop = [(2 * ring[i], 2 * ring[(i + 1) % chips]) for i in range(chips)]
    hop += [(2 * ring[(i + 1) % chips] + 1, 2 * ring[i] + 1) for i in range(chips)]
    swap = [(i, i ^ 1) for i in range(devices)]

    def forward(v):
        return lax.ppermute(v, "expert", hop)

    def other(v):
        return lax.ppermute(v, "expert", swap)

    me = lax.axis_index("expert").reshape(1)
    expert_ids = jnp.arange(devices, dtype=jnp.int32)
    named = routes[:, :, None] == expert_ids[None, None, :]
    probs = jnp.sum(jnp.where(named, gate_probs[:, :, None], 0.0), axis=1)
    x = jnp.concatenate([tokens, encode(probs)], axis=1)
    o = out_grad
    wd = w_down[0]

    def after(v, *others):
        return lax.optimization_barrier((v, *others))[0]

    acc, total, own, back = None, None, None, None
    sums, backs, held = [], [], []
    for s in range(chips):
        if s:
            x = forward(x)
            o = forward(o)
        ties = [o] if s else []
        if s == 1:
            ties += [backs[0]]
        if resident and s == chips - 1 and acc:
            ties += acc
        xo = other(after(x, *ties))
        oo = other(o)
        if s == 0:
            pair = lax.optimization_barrier((w_gate[0], w_up[0], xo))[:2]
            wgu = jnp.concatenate(pair, axis=1)
            o, wgu = lax.optimization_barrier((o, wgu))
        row_a, row_b, grads, hidden = block_pair(me, devices, x, xo, o, oo, wgu, wd)
        backs.append(row_b)
        partial = row_a.astype(F32) + other(row_b).astype(F32)
        if s == 0:
            own = partial
        else:
            if total is not None:
                partial = forward(total).astype(F32) + partial
            total = partial.astype(BF16)
            sums.append(total)
        held.append((x, xo, o, oo, grads, hidden))
        if len(held) == GROUP or s == chips - 1:
            acc = wgrad_group(
                [v for h in held for v in h[:2]],
                [v for h in held for v in h[2:4]],
                [h[4] for h in held],
                [h[5] for h in held],
                acc,
                s == chips - 1,
                resident,
            )
            held = []
            if not resident:
                x, o, acc = lax.optimization_barrier((x, o, acc))
    total = forward(total).astype(F32) + own if chips > 1 else own
    gate_wgrad, up_wgrad, down_wgrad = acc
    return (
        total.astype(BF16),
        gate_wgrad[None],
        up_wgrad[None],
        down_wgrad[None],
    )


def solution(mesh):
    ladder = mesh.shape["groups"] == 2
    rows = P(("groups", "expert"), None)
    weights = P("expert", None, None)
    wgrads = P(("groups", "expert"), None, None)
    return jax.shard_map(
        functools.partial(local, ladder),
        mesh=mesh,
        in_specs=(rows, rows, rows, rows, weights, weights, weights),
        out_specs=(rows, wgrads, wgrads, wgrads),
        check_vma=False,
    )
```

```python
import functools

import jax
import jax.numpy as jnp
from jax import lax
from jax.experimental import pallas as pl
from jax.experimental.pallas import tpu as pltpu
from jax.sharding import PartitionSpec as P

F32 = jnp.float32
BF16 = jnp.bfloat16
NN = (((1,), (0,)), ((), ()))
NT = (((1,), (1,)), ((), ()))
TN = (((0,), (0,)), ((), ()))
GROUP = 4
PARTS = 3
TIES = {'xo': (('o', 0), ('sum', 3)), 'ohop': (('back', 2),)}
LATE = 6
LATE_TIES = {'xo': (('o', 0), ('sum', 3)), 'ohop': (('back', 2),)}
OWN_AT = 'xo'
WGRAD_AT = 'ohop'
WGRAD_STEP = 7
GROUPS = (5, 8)
LAST_PIECES = 1
BLOCK_COST = 4
WGRAD_COST = 1
BLOCK_VMEM = 16 << 20
WGRAD_VMEM = 24 << 20


def mm(a, b, dims):
    return lax.dot_general(a, b, dims, preferred_element_type=F32)


def near(v):
    return pltpu.with_memory_space_constraint(v, pltpu.VMEM)


def encode(probs):
    parts = []
    rest = probs
    for _ in range(PARTS):
        top = lax.reduce_precision(rest, 8, 7)
        parts.append(top.astype(BF16))
        rest = rest - top
    coded = jnp.concatenate(parts, axis=1)
    return jnp.pad(coded, ((0, 0), (0, -coded.shape[1] % 128)))


def block_pair(me, devices, xa, xb, oa, ob, wgu, wd):
    rows, width = oa.shape
    ff = wd.shape[0]

    def body(me, xa, xb, oa, ob, wgu, wd, row_a, row_b, grads, hidden):
        x = jnp.concatenate([xa[:, :width], xb[:, :width]], axis=0)
        o = jnp.concatenate([oa[...], ob[...]], axis=0)
        coded = jnp.concatenate([xa[:, width:], xb[:, width:]], axis=0).astype(F32)
        lane = lax.broadcasted_iota(jnp.int32, coded.shape, 1)
        mine = (lane % devices == me[0]) & (lane < PARTS * devices)
        p = jnp.sum(jnp.where(mine, coded, 0.0), axis=1, keepdims=True)
        pre = mm(x, wgu[...], NN)
        gate, up = pre[:, :ff], pre[:, ff:]
        hid = mm((p * o.astype(F32)).astype(BF16), wd[...], NT)
        sig = jax.nn.sigmoid(gate)
        act = gate * sig
        hidden[...] = (p * (act * up)).astype(BF16)
        grads[:, :ff] = (hid * up * sig * (1.0 + gate * (1.0 - sig))).astype(BF16)
        grads[:, ff:] = (hid * act).astype(BF16)
        back = mm(grads[...], wgu[...], NT).astype(BF16)
        row_a[...] = back[:rows]
        row_b[...] = back[rows:]

    return pl.pallas_call(
        body,
        in_specs=[pl.BlockSpec(memory_space=pltpu.SMEM)]
        + [pl.BlockSpec(memory_space=pltpu.VMEM)] * 6,
        out_shape=[
            jax.ShapeDtypeStruct((rows, width), BF16),
            jax.ShapeDtypeStruct((rows, width), BF16),
            jax.ShapeDtypeStruct((2 * rows, 2 * ff), BF16),
            jax.ShapeDtypeStruct((2 * rows, ff), BF16),
        ],
        compiler_params=pltpu.CompilerParams(vmem_limit_bytes=BLOCK_VMEM),
        cost_estimate=pl.CostEstimate(
            flops=BLOCK_COST * 2 * (2 * rows) * width * ff * 5,
            bytes_accessed=2 * (6 * rows * width + 3 * width * ff),
            transcendentals=2 * rows * ff,
        ),
        name="block_pair",
    )(me, near(xa), near(xb), near(oa), near(ob), near(wgu), near(wd))


def wgrad_group(xs, os, grads, hiddens, acc, last, resident):
    count, pairs = len(xs), len(grads)
    rows, width = os[0].shape
    ff = hiddens[0].shape[1]
    chunk = 512 if resident else 256
    has = acc is not None

    def body(*refs):
        start = pl.multiple_of(pl.program_id(0) * chunk, chunk)
        columns = pl.ds(start, chunk) if resident else slice(None)
        x = jnp.concatenate([r[:, columns] for r in refs[:count]], axis=0)
        o = jnp.concatenate([r[:, columns] for r in refs[count : 2 * count]], axis=0)
        rest = refs[2 * count :]
        g = jnp.concatenate([r[...] for r in rest[:pairs]], axis=0)
        h = jnp.concatenate([r[...] for r in rest[pairs : 2 * pairs]], axis=0)
        rest = rest[2 * pairs :]
        gu = mm(x, g, TN)
        dn = mm(h, o, TN)
        parts = [gu[:, :ff], gu[:, ff:], dn]
        if has:
            parts = [a[...] + b for a, b in zip(rest[:3], parts)]
            rest = rest[3:]
        for r, v in zip(rest, parts):
            r[...] = v.astype(r.dtype)

    tall = pl.BlockSpec((chunk, ff), lambda j: (j, 0))
    wide = pl.BlockSpec((ff, chunk), lambda j: (0, j))
    kind = BF16 if last else F32
    acc_specs = [tall, tall, wide]
    if resident:
        inputs = [near(v) for v in (*xs, *os, *grads, *hiddens)]
        specs = [pl.BlockSpec(memory_space=pltpu.VMEM)] * len(inputs)
    else:
        inputs = [*xs, *os, *grads, *hiddens]
        specs = [
            pl.BlockSpec((v.shape[0], chunk), lambda j: (0, j)) for v in (*xs, *os)
        ]
        specs += [pl.BlockSpec(v.shape, lambda j: (0, 0)) for v in (*grads, *hiddens)]
    alias = {len(inputs) + i: i for i in range(3)} if has and not last else {}
    return pl.pallas_call(
        body,
        grid=(width // chunk,),
        in_specs=specs + (acc_specs if has else []),
        out_specs=acc_specs,
        out_shape=[
            jax.ShapeDtypeStruct((width, ff), kind),
            jax.ShapeDtypeStruct((width, ff), kind),
            jax.ShapeDtypeStruct((ff, width), kind),
        ],
        input_output_aliases=alias,
        compiler_params=pltpu.CompilerParams(vmem_limit_bytes=WGRAD_VMEM),
        cost_estimate=pl.CostEstimate(
            flops=WGRAD_COST * 2 * count * rows * width * ff * 3,
            bytes_accessed=2 * 2 * count * rows * width + 4 * 3 * width * ff,
            transcendentals=0,
        ),
        name="wgrad_group",
    )(*inputs, *(acc if has else ()))


def chip_ring(chips, ladder):
    if ladder:
        return list(range(0, chips, 2)) + list(range(chips - 1, 0, -2))
    return list(range(chips))


def local(ladder, tokens, out_grad, gate_probs, routes, w_gate, w_up, w_down):
    devices = lax.axis_size("expert")
    chips = devices // 2
    resident = chips <= 8
    ring = chip_ring(chips, ladder)
    hop = [(2 * ring[i], 2 * ring[(i + 1) % chips]) for i in range(chips)]
    hop += [(2 * ring[(i + 1) % chips] + 1, 2 * ring[i] + 1) for i in range(chips)]
    swap = [(i, i ^ 1) for i in range(devices)]

    def forward(v):
        return lax.ppermute(v, "expert", hop)

    def other(v):
        return lax.ppermute(v, "expert", swap)

    me = lax.axis_index("expert").reshape(1)
    expert_ids = jnp.arange(devices, dtype=jnp.int32)
    named = routes[:, :, None] == expert_ids[None, None, :]
    probs = jnp.sum(jnp.where(named, gate_probs[:, :, None], 0.0), axis=1)
    x = jnp.concatenate([tokens, encode(probs)], axis=1)
    o = out_grad
    wd = w_down[0]

    def after(v, *others):
        return lax.optimization_barrier((v, *others))[0] if others else v

    acc, total, own = None, None, None
    sums, backs, xs_seen, os_seen, held = [], [], [], [], []

    def ties_for(name, s):
        found = []
        for kind, lag in TIES.get(name, ()) if s < LATE else LATE_TIES.get(name, ()):
            seen = {"sum": sums, "back": backs, "x": xs_seen, "o": os_seen}[kind]
            index = s - lag
            if 0 <= index < len(seen):
                found.append(seen[index])
        if name == OWN_AT and s == 1:
            found.append(backs[0])
        if resident and acc is not None and name == WGRAD_AT and s == WGRAD_STEP:
            found.extend(acc)
        return found

    for s in range(chips):
        pieces = [(x, o)]
        if s:
            x = after(x, *ties_for("xhop", s))
            o = after(o, *ties_for("ohop", s))
            count = LAST_PIECES if s == chips - 1 else 1
            pieces = [
                (forward(a), forward(b))
                for a, b in zip(jnp.split(x, count), jnp.split(o, count))
            ]
        x, o = pieces[0]
        partial = []
        for k, (x, o) in enumerate(pieces):
            xs_seen.append(x)
            os_seen.append(o)
            xo = other(after(x, *ties_for("xo", s + k)) if s else x)
            oo = other(after(o, *ties_for("oo", s + k)) if s else o)
            if s == 0:
                pair = lax.optimization_barrier((w_gate[0], w_up[0], xo))[:2]
                wgu = jnp.concatenate(pair, axis=1)
                o, wgu = lax.optimization_barrier((o, wgu))
            row_a, row_b, grads, hidden = block_pair(
                me, devices, x, xo, o, after(oo, *ties_for("block", s + k)), wgu, wd
            )
            backs.append(row_b)
            partial.append(row_a.astype(F32) + other(row_b).astype(F32))
            held.append((x, xo, o, oo, grads, hidden))
        if s == 0:
            own = partial[0]
        else:
            if total is not None:
                came = forward(after(total, *ties_for("rs", s))).astype(F32)
                parts = jnp.split(came, len(partial))
                partial = [a + b for a, b in zip(parts, partial)]
            total = partial[0].astype(BF16)
            sums.append(total)
        if (s + 1 in GROUPS) if resident else (len(held) >= GROUP or s == chips - 1):
            acc = wgrad_group(
                [v for h in held for v in h[:2]],
                [v for h in held for v in h[2:4]],
                [h[4] for h in held],
                [h[5] for h in held],
                acc,
                s == chips - 1,
                resident,
            )
            held = []
            if not resident:
                x, o, acc = lax.optimization_barrier((x, o, acc))
    total = [forward(p.astype(BF16)) for p in partial]
    total = jnp.concatenate(total, axis=0).astype(F32) + own
    gate_wgrad, up_wgrad, down_wgrad = acc
    return (
        total.astype(BF16),
        gate_wgrad[None],
        up_wgrad[None],
        down_wgrad[None],
    )


def solution(mesh):
    ladder = mesh.shape["groups"] == 2
    rows = P(("groups", "expert"), None)
    weights = P("expert", None, None)
    wgrads = P(("groups", "expert"), None, None)
    return jax.shard_map(
        functools.partial(local, ladder),
        mesh=mesh,
        in_specs=(rows, rows, rows, rows, weights, weights, weights),
        out_specs=(rows, wgrads, wgrads, wgrads),
        check_vma=False,
    )
```

```python
import functools

import jax
import jax.numpy as jnp
from jax import lax
from jax.experimental import pallas as pl
from jax.experimental.pallas import tpu as pltpu
from jax.sharding import PartitionSpec as P

F32 = jnp.float32
BF16 = jnp.bfloat16
NN = (((1,), (0,)), ((), ()))
NT = (((1,), (1,)), ((), ()))
TN = (((0,), (0,)), ((), ()))
GROUP = 4
PARTS = 3
TIES = {'xo': (('o', 0), ('sum', 3)), 'ohop': (('back', 2),)}
OWN_AT = 'xo'
WGRAD_TIES = ((0, 'block', 6),)
GROUPS = (5, 8)
BLOCK_COST = 16
WGRAD_COST = 1
BLOCK_VMEM = 16 << 20
WGRAD_VMEM = 24 << 20


def mm(a, b, dims):
    return lax.dot_general(a, b, dims, preferred_element_type=F32)


def near(v):
    return pltpu.with_memory_space_constraint(v, pltpu.VMEM)


def encode(probs):
    parts = []
    rest = probs
    for _ in range(PARTS):
        top = lax.reduce_precision(rest, 8, 7)
        parts.append(top.astype(BF16))
        rest = rest - top
    coded = jnp.concatenate(parts, axis=1)
    return jnp.pad(coded, ((0, 0), (0, -coded.shape[1] % 128)))


def block_pair(me, devices, xa, xb, oa, ob, wgu, wd):
    rows, width = oa.shape
    ff = wd.shape[0]

    def body(me, xa, xb, oa, ob, wgu, wd, row_a, row_b, grads, hidden):
        x = jnp.concatenate([xa[:, :width], xb[:, :width]], axis=0)
        o = jnp.concatenate([oa[...], ob[...]], axis=0)
        coded = jnp.concatenate([xa[:, width:], xb[:, width:]], axis=0).astype(F32)
        lane = lax.broadcasted_iota(jnp.int32, coded.shape, 1)
        mine = (lane % devices == me[0]) & (lane < PARTS * devices)
        p = jnp.sum(jnp.where(mine, coded, 0.0), axis=1, keepdims=True)
        pre = mm(x, wgu[...], NN)
        gate, up = pre[:, :ff], pre[:, ff:]
        hid = mm((p * o.astype(F32)).astype(BF16), wd[...], NT)
        sig = jax.nn.sigmoid(gate)
        act = gate * sig
        hidden[...] = (p * (act * up)).astype(BF16)
        grads[:, :ff] = (hid * up * sig * (1.0 + gate * (1.0 - sig))).astype(BF16)
        grads[:, ff:] = (hid * act).astype(BF16)
        back = mm(grads[...], wgu[...], NT).astype(BF16)
        row_a[...] = back[:rows]
        row_b[...] = back[rows:]

    return pl.pallas_call(
        body,
        in_specs=[pl.BlockSpec(memory_space=pltpu.SMEM)]
        + [pl.BlockSpec(memory_space=pltpu.VMEM)] * 6,
        out_shape=[
            jax.ShapeDtypeStruct((rows, width), BF16),
            jax.ShapeDtypeStruct((rows, width), BF16),
            jax.ShapeDtypeStruct((2 * rows, 2 * ff), BF16),
            jax.ShapeDtypeStruct((2 * rows, ff), BF16),
        ],
        compiler_params=pltpu.CompilerParams(vmem_limit_bytes=BLOCK_VMEM),
        cost_estimate=pl.CostEstimate(
            flops=BLOCK_COST * 2 * (2 * rows) * width * ff * 5,
            bytes_accessed=2 * (6 * rows * width + 3 * width * ff),
            transcendentals=2 * rows * ff,
        ),
        name="block_pair",
    )(me, near(xa), near(xb), near(oa), near(ob), near(wgu), near(wd))


def wgrad_group(xs, os, grads, hiddens, acc, last, resident):
    count, pairs = len(xs), len(grads)
    rows, width = os[0].shape
    ff = hiddens[0].shape[1]
    chunk = 512 if resident else 256
    has = acc is not None

    def body(*refs):
        start = pl.multiple_of(pl.program_id(0) * chunk, chunk)
        columns = pl.ds(start, chunk) if resident else slice(None)
        x = jnp.concatenate([r[:, columns] for r in refs[:count]], axis=0)
        o = jnp.concatenate([r[:, columns] for r in refs[count : 2 * count]], axis=0)
        rest = refs[2 * count :]
        g = jnp.concatenate([r[...] for r in rest[:pairs]], axis=0)
        h = jnp.concatenate([r[...] for r in rest[pairs : 2 * pairs]], axis=0)
        rest = rest[2 * pairs :]
        gu = mm(x, g, TN)
        dn = mm(h, o, TN)
        parts = [gu[:, :ff], gu[:, ff:], dn]
        if has:
            parts = [a[...] + b for a, b in zip(rest[:3], parts)]
            rest = rest[3:]
        for r, v in zip(rest, parts):
            r[...] = v.astype(r.dtype)

    tall = pl.BlockSpec((chunk, ff), lambda j: (j, 0))
    wide = pl.BlockSpec((ff, chunk), lambda j: (0, j))
    kind = BF16 if last else F32
    acc_specs = [tall, tall, wide]
    if resident:
        inputs = [near(v) for v in (*xs, *os, *grads, *hiddens)]
        specs = [pl.BlockSpec(memory_space=pltpu.VMEM)] * len(inputs)
    else:
        inputs = [*xs, *os, *grads, *hiddens]
        specs = [
            pl.BlockSpec((v.shape[0], chunk), lambda j: (0, j)) for v in (*xs, *os)
        ]
        specs += [pl.BlockSpec(v.shape, lambda j: (0, 0)) for v in (*grads, *hiddens)]
    alias = {len(inputs) + i: i for i in range(3)} if has and not last else {}
    return pl.pallas_call(
        body,
        grid=(width // chunk,),
        in_specs=specs + (acc_specs if has else []),
        out_specs=acc_specs,
        out_shape=[
            jax.ShapeDtypeStruct((width, ff), kind),
            jax.ShapeDtypeStruct((width, ff), kind),
            jax.ShapeDtypeStruct((ff, width), kind),
        ],
        input_output_aliases=alias,
        compiler_params=pltpu.CompilerParams(vmem_limit_bytes=WGRAD_VMEM),
        cost_estimate=pl.CostEstimate(
            flops=WGRAD_COST * 2 * count * rows * width * ff * 3,
            bytes_accessed=2 * 2 * count * rows * width + 4 * 3 * width * ff,
            transcendentals=0,
        ),
        name="wgrad_group",
    )(*inputs, *(acc if has else ()))


def chip_ring(chips, ladder):
    if ladder:
        return list(range(0, chips, 2)) + list(range(chips - 1, 0, -2))
    return list(range(chips))


def local(ladder, tokens, out_grad, gate_probs, routes, w_gate, w_up, w_down):
    devices = lax.axis_size("expert")
    chips = devices // 2
    resident = chips <= 8
    ring = chip_ring(chips, ladder)
    hop = [(2 * ring[i], 2 * ring[(i + 1) % chips]) for i in range(chips)]
    hop += [(2 * ring[(i + 1) % chips] + 1, 2 * ring[i] + 1) for i in range(chips)]
    swap = [(i, i ^ 1) for i in range(devices)]

    def forward(v):
        return lax.ppermute(v, "expert", hop)

    def other(v):
        return lax.ppermute(v, "expert", swap)

    me = lax.axis_index("expert").reshape(1)
    expert_ids = jnp.arange(devices, dtype=jnp.int32)
    named = routes[:, :, None] == expert_ids[None, None, :]
    probs = jnp.sum(jnp.where(named, gate_probs[:, :, None], 0.0), axis=1)
    x = jnp.concatenate([tokens, encode(probs)], axis=1)
    o = out_grad
    wd = w_down[0]

    def after(v, *others):
        return lax.optimization_barrier((v, *others))[0] if others else v

    acc, total, own = None, None, None
    sums, backs, xs_seen, os_seen, held, accs = [], [], [], [], [], []

    def ties_for(name, s):
        found = []
        for kind, lag in TIES.get(name, ()):
            seen = {"sum": sums, "back": backs, "x": xs_seen, "o": os_seen}[kind]
            index = s - lag
            if 0 <= index < len(seen):
                found.append(seen[index])
        if name == OWN_AT and s == 1:
            found.append(backs[0])
        for group, place, step in WGRAD_TIES if resident else ():
            if (place, step) == (name, s) and group < len(accs):
                found.extend(accs[group])
        return found

    for s in range(chips):
        if s:
            x = after(x, *ties_for("xhop", s))
            o = after(o, *ties_for("ohop", s))
            x, o = forward(x), forward(o)
        xs_seen.append(x)
        os_seen.append(o)
        xo = other(after(x, *ties_for("xo", s)) if s else x)
        oo = other(after(o, *ties_for("oo", s)) if s else o)
        if s == 0:
            pair = lax.optimization_barrier((w_gate[0], w_up[0], xo))[:2]
            wgu = jnp.concatenate(pair, axis=1)
            o, wgu = lax.optimization_barrier((o, wgu))
        row_a, row_b, grads, hidden = block_pair(
            me, devices, x, xo, o, after(oo, *ties_for("block", s)), wgu, wd
        )
        backs.append(row_b)
        held.append((x, xo, o, oo, grads, hidden))
        if s == chips - 1 and chips > 2:
            row_a, row_b, late = lax.optimization_barrier((row_a, row_b, late))
            halves = zip(jnp.split(late, 2), jnp.split(owed, 2))
            total = [(a.astype(F32) + b).astype(BF16) for a, b in halves]
        partial = row_a.astype(F32) + other(row_b).astype(F32)
        if s == 0:
            own = partial
        elif s == chips - 2 and s > 1:
            late, owed = forward(after(total, *ties_for("rs", s))), partial
        elif s == chips - 1 and chips > 2:
            top, low = [forward(t) for t in total]
            top_part, low_part = jnp.split(partial, 2)
            top = (top.astype(F32) + top_part).astype(BF16)
            low = (after(low, top).astype(F32) + low_part).astype(BF16)
            total = jnp.concatenate([forward(top), forward(low)], axis=0)
        else:
            if total is not None:
                came = forward(after(total, *ties_for("rs", s)))
                partial = came.astype(F32) + partial
            total = partial.astype(BF16)
            sums.append(total)
        if (s + 1 in GROUPS) if resident else (len(held) >= GROUP or s == chips - 1):
            acc = wgrad_group(
                [v for h in held for v in h[:2]],
                [v for h in held for v in h[2:4]],
                [h[4] for h in held],
                [h[5] for h in held],
                acc,
                s == chips - 1,
                resident,
            )
            held = []
            accs.append(acc)
            if not resident:
                x, o, acc = lax.optimization_barrier((x, o, acc))
    if chips <= 2:
        total = forward(total)
    total = total.astype(F32) + own
    gate_wgrad, up_wgrad, down_wgrad = acc
    return (
        total.astype(BF16),
        gate_wgrad[None],
        up_wgrad[None],
        down_wgrad[None],
    )


def solution(mesh):
    ladder = mesh.shape["groups"] == 2
    rows = P(("groups", "expert"), None)
    weights = P("expert", None, None)
    wgrads = P(("groups", "expert"), None, None)
    return jax.shard_map(
        functools.partial(local, ladder),
        mesh=mesh,
        in_specs=(rows, rows, rows, rows, weights, weights, weights),
        out_specs=(rows, wgrads, wgrads, wgrads),
        check_vma=False,
    )
```

```python
import functools

import jax
import jax.numpy as jnp
from jax import lax
from jax.experimental import pallas as pl
from jax.experimental.pallas import tpu as pltpu
from jax.sharding import PartitionSpec as P

F32 = jnp.float32
BF16 = jnp.bfloat16
NN = (((1,), (0,)), ((), ()))
NT = (((1,), (1,)), ((), ()))
TN = (((0,), (0,)), ((), ()))
GROUP = 4
PARTS = 3
TIES = {'xo': (('o', 0), ('sum', 3)), 'ohop': (('back', 2),)}
OWN_AT = 'xo'
WGRAD_TIES = ((0, 'block', 6),)
GROUPS = (5, 8)
BLOCK_COST = 16
WGRAD_COST = 1
BLOCK_VMEM = 16 << 20
WGRAD_VMEM = 28 << 20


def mm(a, b, dims):
    return lax.dot_general(a, b, dims, preferred_element_type=F32)


def near(v):
    return pltpu.with_memory_space_constraint(v, pltpu.VMEM)


def encode(probs):
    parts = []
    rest = probs
    for _ in range(PARTS):
        top = lax.reduce_precision(rest, 8, 7)
        parts.append(top.astype(BF16))
        rest = rest - top
    coded = jnp.concatenate(parts, axis=1)
    return jnp.pad(coded, ((0, 0), (0, -coded.shape[1] % 128)))


def block_pair(me, devices, xa, xb, oa, ob, wgu, wd):
    rows, width = oa.shape
    ff = wd.shape[0]

    def body(me, xa, xb, oa, ob, wgu, wd, row_a, row_b, grads, hidden):
        x = jnp.concatenate([xa[:, :width], xb[:, :width]], axis=0)
        o = jnp.concatenate([oa[...], ob[...]], axis=0)
        coded = jnp.concatenate([xa[:, width:], xb[:, width:]], axis=0).astype(F32)
        lane = lax.broadcasted_iota(jnp.int32, coded.shape, 1)
        mine = (lane % devices == me[0]) & (lane < PARTS * devices)
        p = jnp.sum(jnp.where(mine, coded, 0.0), axis=1, keepdims=True)
        pre = mm(x, wgu[...], NN)
        gate, up = pre[:, :ff], pre[:, ff:]
        hid = mm((p * o.astype(F32)).astype(BF16), wd[...], NT)
        sig = jax.nn.sigmoid(gate)
        act = gate * sig
        hidden[...] = (p * (act * up)).astype(BF16)
        grads[:, :ff] = (hid * up * sig * (1.0 + gate * (1.0 - sig))).astype(BF16)
        grads[:, ff:] = (hid * act).astype(BF16)
        back = mm(grads[...], wgu[...], NT).astype(BF16)
        row_a[...] = back[:rows]
        row_b[...] = back[rows:]

    return pl.pallas_call(
        body,
        in_specs=[pl.BlockSpec(memory_space=pltpu.SMEM)]
        + [pl.BlockSpec(memory_space=pltpu.VMEM)] * 6,
        out_shape=[
            jax.ShapeDtypeStruct((rows, width), BF16),
            jax.ShapeDtypeStruct((rows, width), BF16),
            jax.ShapeDtypeStruct((2 * rows, 2 * ff), BF16),
            jax.ShapeDtypeStruct((2 * rows, ff), BF16),
        ],
        compiler_params=pltpu.CompilerParams(vmem_limit_bytes=BLOCK_VMEM),
        cost_estimate=pl.CostEstimate(
            flops=BLOCK_COST * 2 * (2 * rows) * width * ff * 5,
            bytes_accessed=2 * (6 * rows * width + 3 * width * ff),
            transcendentals=2 * rows * ff,
        ),
        name="block_pair",
    )(me, near(xa), near(xb), near(oa), near(ob), near(wgu), near(wd))


def wgrad_group(xs, os, grads, hiddens, acc, last, resident):
    count, pairs = len(xs), len(grads)
    rows, width = os[0].shape
    ff = hiddens[0].shape[1]
    chunk = 1024 if resident else 256
    has = acc is not None

    def body(*refs):
        start = pl.multiple_of(pl.program_id(0) * chunk, chunk)
        columns = pl.ds(start, chunk) if resident else slice(None)
        x = jnp.concatenate([r[:, columns] for r in refs[:count]], axis=0)
        o = jnp.concatenate([r[:, columns] for r in refs[count : 2 * count]], axis=0)
        rest = refs[2 * count :]
        g = jnp.concatenate([r[...] for r in rest[:pairs]], axis=0)
        h = jnp.concatenate([r[...] for r in rest[pairs : 2 * pairs]], axis=0)
        rest = rest[2 * pairs :]
        gu = mm(x, g, TN)
        dn = mm(h, o, TN)
        parts = [gu[:, :ff], gu[:, ff:], dn]
        if has:
            parts = [a[...] + b for a, b in zip(rest[:3], parts)]
            rest = rest[3:]
        for r, v in zip(rest, parts):
            r[...] = v.astype(r.dtype)

    tall = pl.BlockSpec((chunk, ff), lambda j: (j, 0))
    wide = pl.BlockSpec((ff, chunk), lambda j: (0, j))
    kind = BF16 if last else F32
    acc_specs = [tall, tall, wide]
    if resident:
        inputs = [near(v) for v in (*xs, *os, *grads, *hiddens)]
        specs = [pl.BlockSpec(memory_space=pltpu.VMEM)] * len(inputs)
    else:
        inputs = [*xs, *os, *grads, *hiddens]
        specs = [
            pl.BlockSpec((v.shape[0], chunk), lambda j: (0, j)) for v in (*xs, *os)
        ]
        specs += [pl.BlockSpec(v.shape, lambda j: (0, 0)) for v in (*grads, *hiddens)]
    alias = {len(inputs) + i: i for i in range(3)} if has and not last else {}
    return pl.pallas_call(
        body,
        grid=(width // chunk,),
        in_specs=specs + (acc_specs if has else []),
        out_specs=acc_specs,
        out_shape=[
            jax.ShapeDtypeStruct((width, ff), kind),
            jax.ShapeDtypeStruct((width, ff), kind),
            jax.ShapeDtypeStruct((ff, width), kind),
        ],
        input_output_aliases=alias,
        compiler_params=pltpu.CompilerParams(vmem_limit_bytes=WGRAD_VMEM),
        cost_estimate=pl.CostEstimate(
            flops=WGRAD_COST * 2 * count * rows * width * ff * 3,
            bytes_accessed=2 * 2 * count * rows * width + 4 * 3 * width * ff,
            transcendentals=0,
        ),
        name="wgrad_group",
    )(*inputs, *(acc if has else ()))


def chip_ring(chips, ladder):
    if ladder:
        return list(range(0, chips, 2)) + list(range(chips - 1, 0, -2))
    return list(range(chips))


def local(ladder, tokens, out_grad, gate_probs, routes, w_gate, w_up, w_down):
    devices = lax.axis_size("expert")
    chips = devices // 2
    resident = chips <= 8
    ring = chip_ring(chips, ladder)
    hop = [(2 * ring[i], 2 * ring[(i + 1) % chips]) for i in range(chips)]
    hop += [(2 * ring[(i + 1) % chips] + 1, 2 * ring[i] + 1) for i in range(chips)]
    swap = [(i, i ^ 1) for i in range(devices)]

    def forward(v):
        return lax.ppermute(v, "expert", hop)

    def other(v):
        return lax.ppermute(v, "expert", swap)

    me = lax.axis_index("expert").reshape(1)
    expert_ids = jnp.arange(devices, dtype=jnp.int32)
    named = routes[:, :, None] == expert_ids[None, None, :]
    probs = jnp.sum(jnp.where(named, gate_probs[:, :, None], 0.0), axis=1)
    x = jnp.concatenate([tokens, encode(probs)], axis=1)
    o = out_grad
    wd = w_down[0]

    def after(v, *others):
        return lax.optimization_barrier((v, *others))[0] if others else v

    acc, total, own = None, None, None
    sums, backs, xs_seen, os_seen, held, accs = [], [], [], [], [], []

    def ties_for(name, s):
        found = []
        for kind, lag in TIES.get(name, ()):
            seen = {"sum": sums, "back": backs, "x": xs_seen, "o": os_seen}[kind]
            index = s - lag
            if 0 <= index < len(seen):
                found.append(seen[index])
        if name == OWN_AT and s == 1:
            found.append(backs[0])
        for group, place, step in WGRAD_TIES if resident else ():
            if (place, step) == (name, s) and group < len(accs):
                found.extend(accs[group])
        return found

    for s in range(chips):
        if s:
            x = after(x, *ties_for("xhop", s))
            o = after(o, *ties_for("ohop", s))
            x, o = forward(x), forward(o)
        xs_seen.append(x)
        os_seen.append(o)
        xo = other(after(x, *ties_for("xo", s)) if s else x)
        oo = other(after(o, *ties_for("oo", s)) if s else o)
        if s == 0:
            pair = lax.optimization_barrier((w_gate[0], w_up[0], xo))[:2]
            wgu = jnp.concatenate(pair, axis=1)
            o, wgu = lax.optimization_barrier((o, wgu))
        row_a, row_b, grads, hidden = block_pair(
            me, devices, x, xo, o, after(oo, *ties_for("block", s)), wgu, wd
        )
        backs.append(row_b)
        held.append((x, xo, o, oo, grads, hidden))
        if s == chips - 1 and chips > 2:
            row_a, row_b, late = lax.optimization_barrier((row_a, row_b, late))
            halves = zip(jnp.split(late, 2), jnp.split(owed, 2))
            total = [(a.astype(F32) + b).astype(BF16) for a, b in halves]
        partial = row_a.astype(F32) + other(row_b).astype(F32)
        if s == 0:
            own = partial
        elif s == chips - 2 and s > 1:
            late, owed = forward(after(total, *ties_for("rs", s))), partial
        elif s == chips - 1 and chips > 2:
            top, low = [forward(t) for t in total]
            top_part, low_part = jnp.split(partial, 2)
            top = (top.astype(F32) + top_part).astype(BF16)
            low = (after(low, top).astype(F32) + low_part).astype(BF16)
            total = jnp.concatenate([forward(top), forward(low)], axis=0)
        else:
            if total is not None:
                came = forward(after(total, *ties_for("rs", s)))
                partial = came.astype(F32) + partial
            total = partial.astype(BF16)
            sums.append(total)
        if (s + 1 in GROUPS) if resident else (len(held) >= GROUP or s == chips - 1):
            acc = wgrad_group(
                [v for h in held for v in h[:2]],
                [v for h in held for v in h[2:4]],
                [h[4] for h in held],
                [h[5] for h in held],
                acc,
                s == chips - 1,
                resident,
            )
            held = []
            accs.append(acc)
            if not resident:
                x, o, acc = lax.optimization_barrier((x, o, acc))
    if chips <= 2:
        total = forward(total)
    total = total.astype(F32) + own
    gate_wgrad, up_wgrad, down_wgrad = acc
    return (
        total.astype(BF16),
        gate_wgrad[None],
        up_wgrad[None],
        down_wgrad[None],
    )


def solution(mesh):
    ladder = mesh.shape["groups"] == 2
    rows = P(("groups", "expert"), None)
    weights = P("expert", None, None)
    wgrads = P(("groups", "expert"), None, None)
    return jax.shard_map(
        functools.partial(local, ladder),
        mesh=mesh,
        in_specs=(rows, rows, rows, rows, weights, weights, weights),
        out_specs=(rows, wgrads, wgrads, wgrads),
        check_vma=False,
    )
```
